32 devices in a mesh: row: 8 (over z, x), col: 4 (over y, core).
Axes of the slice: x: 2, y: 2, z: 4, core: 2. Of those that a mesh axis runs over, the one named last changes fastest.
Arguments:
- image_tokens: bfloat16 [8192, 1536], P('row', 'col'), may hold values from -40 to 40
- text_tokens: bfloat16 [1232, 1536], P('row', 'col'), may hold values from -40 to 40
- conditioning: bfloat16 [8, 1536], P('row'), may hold values from -6 to 6
- text_valid: int32 [8, 154], P('row'), may hold values 0 or 1
- image_modulation: bfloat16 [1536, 6, 1536], P('row', None, 'col'), may hold values from -0.15625 to 0.15625
- text_modulation: bfloat16 [1536, 6, 1536], P('row', None, 'col'), may hold values from -0.15625 to 0.15625
- image_inward: bfloat16 [1536, 3, 1536], P('row', None, 'col'), may hold values from -1 to 1
- text_inward: bfloat16 [1536, 3, 1536], P('row', None, 'col'), may hold values from -1 to 1
- image_outward: bfloat16 [1536, 1536], P('col', 'row'), may hold values from -0.4375 to 0.4375
- text_outward: bfloat16 [1536, 1536], P('col', 'row'), may hold values from -0.4375 to 0.4375
- image_expand: bfloat16 [1536, 6144], P('row', 'col'), may hold values from -0.15625 to 0.15625
- text_expand: bfloat16 [1536, 6144], P('row', 'col'), may hold values from -0.15625 to 0.15625
- image_contract: bfloat16 [6144, 1536], P('col', 'row'), may hold values from -0.078125 to 0.078125
- text_contract: bfloat16 [6144, 1536], P('col', 'row'), may hold values from -0.078125 to 0.078125
- image_cotangent: bfloat16 [8192, 1536], P('row', 'col'), may hold values from -6 to 6
- text_cotangent: bfloat16 [1232, 1536], P('row', 'col'), may hold values from -6 to 6
Outputs:
- image_output: bfloat16 [8192, 1536], P('row', 'col')
- text_output: bfloat16 [1232, 1536], P('row', 'col')
- image_input_grad: float32 [8192, 1536], P('row', 'col')
- text_input_grad: float32 [1232, 1536], P('row', 'col')
- grad_image_modulation: float32 [1536, 6, 1536], P('row', None, 'col')
- grad_text_modulation: float32 [1536, 6, 1536], P('row', None, 'col')
- grad_image_inward: float32 [1536, 3, 1536], P('row', None, 'col')
- grad_text_inward: float32 [1536, 3, 1536], P('row', None, 'col')
- grad_image_outward: float32 [1536, 1536], P('col', 'row')
- grad_text_outward: float32 [1536, 1536], P('col', 'row')
- grad_image_expand: float32 [1536, 6144], P('row', 'col')
- grad_text_expand: float32 [1536, 6144], P('row', 'col')
- grad_image_contract: float32 [6144, 1536], P('col', 'row')
- grad_text_contract: float32 [6144, 1536], P('col', 'row')
The draws below stay inside these ranges and needn't reach their ends.
All inputs are finite; a program needn't handle non-finite values. No bound on the sum of `text_valid` on one device may be relied on, other than what follows from the above.
Results may differ from the reference program's by a relative error of at most 0.0361.
The reference program's roundings to bfloat16 on the way count: a program that leaves them out, or rounds other values in their place, can miss the bound.
Values may be sent and summed in bfloat16 or wider, within the bound.
No kernel may reach another device: no remote copies, remote signals or barrier semaphores. Data moves between devices by JAX's collectives and lax.ppermute only.
A program may use at most 256 MiB of HBM per device.

```python
import math
import jax
import jax.numpy as jnp
from jax import lax

D = 1536
H = 24
HD = 64
FF = 6144
LI = 1024
LT = 154
SEQS = 8


def token_values(key, row_count):
    base_key, row_key, column_key = jax.random.split(key, 3)
    ramp = jnp.exp(jnp.arange(D, dtype=jnp.float32) * (math.log(3.0) / D))
    column_scale = ramp[None, :] * jnp.exp(jax.random.uniform(column_key, (1, D), jnp.float32, -0.6, 0.6)) / 1.8
    row_scale = jnp.exp(jax.random.uniform(row_key, (row_count, 1), jnp.float32, math.log(0.3), math.log(3.0)))
    values = jax.random.truncated_normal(base_key, -4.0, 4.0, (row_count, D), jnp.float32)
    return values * row_scale * column_scale


def draw_image_tokens(key, part):
    return token_values(jax.random.fold_in(key, 101), SEQS * LI).astype(jnp.bfloat16)


def draw_text_tokens(key, part):
    return token_values(jax.random.fold_in(key, 202), SEQS * LT).astype(jnp.bfloat16)


def inward_values(key):
    values = jax.random.truncated_normal(key, -4.0, 4.0, (D, 3, D), jnp.float32) / math.sqrt(D)
    return values


def draw_image_inward(key, part):
    return inward_values(jax.random.fold_in(key, 303)).astype(jnp.bfloat16)


def draw_text_inward(key, part):
    return inward_values(jax.random.fold_in(key, 404)).astype(jnp.bfloat16)


def plant(array, stream_key, smallest, top_value):
    index_at = [jax.random.randint(jax.random.fold_in(stream_key, axis), (), 0, length) for axis, length in enumerate(array.shape)]
    widest = array.shape.index(max(array.shape))
    neighbour = index_at[:widest] + [(index_at[widest] + 1) % array.shape[widest]] + index_at[widest + 1:]
    return array.at[tuple(index_at)].set(smallest).at[tuple(neighbour)].set(top_value)


def spiked(drawn, stream_key, source, target, shards_of, factor):
    def block_of(axis_at):
        return (jnp.arange(drawn.shape[axis_at]) // (drawn.shape[axis_at] // shards_of)).reshape((-1,) + (1,) * (drawn.ndim - 1 - axis_at))

    near = jax.random.permutation(stream_key, shards_of)[block_of(target)]
    far = (block_of(target) + shards_of // 2) % shards_of
    return jnp.where((block_of(source) == near) | (block_of(source) == far), factor * drawn, drawn)


def levels(rng, extent, cuts, smallest, high):
    loudness = 1.0
    for dim, blocks in cuts:
        heights = jax.random.uniform(jax.random.fold_in(jax.random.fold_in(rng, 6), dim), (blocks,), jnp.float32, smallest / len(cuts), high / len(cuts))
        loudness = loudness * jnp.repeat(jnp.exp(heights), extent[dim] // blocks).reshape((-1,) + (1,) * (len(extent) - 1 - dim))
    return loudness


def centred(key, extent, deviation, reach, cuts=(), kind=jnp.bfloat16):
    drawn = deviation * jax.random.normal(key, extent, jnp.float32)
    if cuts:
        drawn = drawn * levels(key, extent, cuts, -0.22, 0.18)
    return jnp.clip(drawn, -reach, reach).astype(kind)


def bell_draw_with(stream_key, extent, scale, most, cuts, heavy, kind=jnp.bfloat16):
    array = scale * jax.random.normal(stream_key, extent, jnp.float32)
    if cuts:
        array = array * levels(stream_key, extent, cuts, -0.22, 0.18)
    return jnp.clip(spiked(array, jax.random.fold_in(stream_key, 3), *heavy), -most, most).astype(kind)


def setup_inputs(seed: int = 0) -> dict:
    key_of = jax.random.split(jax.random.key(seed), 17)
    return {
        "image_tokens": draw_image_tokens(jax.random.fold_in(key_of[16], 71), 0),
        "text_tokens": draw_text_tokens(jax.random.fold_in(key_of[16], 71), 0),
        "conditioning": centred(key_of[2], (SEQS, D), 1.0, 6.0, ((0, 8),)),
        "text_valid": plant((jax.random.randint(key_of[3], (SEQS, LT), 0, 4) < 3).astype(jnp.int32), jax.random.fold_in(key_of[3], 1), 0, 1),
        "image_modulation": centred(key_of[4], (D, 6, D), D ** -0.5, 0.15625, ((0, 8), (2, 4))),
        "text_modulation": centred(key_of[5], (D, 6, D), D ** -0.5, 0.15625, ((0, 8), (2, 4))),
        "image_inward": draw_image_inward(jax.random.fold_in(key_of[16], 71), 0),
        "text_inward": draw_text_inward(jax.random.fold_in(key_of[16], 71), 0),
        "image_outward": centred(key_of[8], (D, D), (D // 8) ** -0.5, 0.4375, ((0, 4), (1, 8))),
        "text_outward": centred(key_of[9], (D, D), (D // 8) ** -0.5, 0.4375, ((0, 4), (1, 8))),
        "image_expand": centred(key_of[10], (D, FF), D ** -0.5, 0.15625, ((0, 8), (1, 4))),
        "text_expand": centred(key_of[11], (D, FF), D ** -0.5, 0.15625, ((0, 8), (1, 4))),
        "image_contract": centred(key_of[12], (FF, D), FF ** -0.5, 0.078125, ((0, 4), (1, 8))),
        "text_contract": centred(key_of[13], (FF, D), FF ** -0.5, 0.078125, ((0, 4), (1, 8))),
        "image_cotangent": bell_draw_with(key_of[14], (SEQS * LI, D), 1.0, 6.0, ((0, 8), (1, 4)), (0, 1, 8, 2.0)),
        "text_cotangent": bell_draw_with(key_of[15], (SEQS * LT, D), 1.0, 6.0, ((0, 8), (1, 4)), (0, 1, 8, 2.0)),
    }


EPSILON = 1e-06
MASKED = -1e+30
GELU_SCALE = 0.7978845608028654
GELU_CUBIC = 0.044715

def gelu_tanh(values):
    return 0.5 * values * (1.0 + jnp.tanh(GELU_SCALE * (values + GELU_CUBIC * values * values * values)))

def gelu_slope(values):
    tangent = jnp.tanh(GELU_SCALE * (values + GELU_CUBIC * values * values * values))
    return 0.5 * (1.0 + tangent) + 0.5 * values * (1.0 - tangent * tangent) * GELU_SCALE * (1.0 + 3.0 * GELU_CUBIC * values * values)

def dense_product(left, right):
    return jnp.dot(left, right, preferred_element_type=jnp.float32)

def normalize(values):
    average = lax.optimization_barrier(jnp.mean(values, axis=-1, keepdims=True))
    squares = lax.optimization_barrier(jnp.mean(values * values, axis=-1, keepdims=True))
    inverse = lax.rsqrt(squares - average * average + EPSILON)
    return ((values - average) * inverse, inverse)

def norm_back(upward, normed, inverse):
    return inverse * (upward - lax.optimization_barrier(jnp.mean(upward, axis=-1, keepdims=True)) - normed * lax.optimization_barrier(jnp.mean(upward * normed, axis=-1, keepdims=True)))

def reference(image_tokens, text_tokens, conditioning, text_valid, image_modulation, text_modulation, image_inward, text_inward, image_outward, text_outward, image_expand, text_expand, image_contract, text_contract, image_cotangent, text_cotangent):
    cond_silu = jax.nn.silu(conditioning.astype(jnp.float32)).astype(jnp.bfloat16)
    tables = (image_modulation.reshape(D, 6 * D), text_modulation.reshape(D, 6 * D))
    modulations = tuple((dense_product(cond_silu, table_part).reshape(SEQS, 6, D) for table_part in tables))
    inward = (image_inward.reshape(D, 3 * D), text_inward.reshape(D, 3 * D))
    outward = (image_outward, text_outward)
    expand = (image_expand, text_expand)
    contract = (image_contract, text_contract)
    lengths = (LI, LT)
    score_scale = HD ** (-0.5)
    joint_len = LI + LT

    def one_sequence(carried, pieces):
        tokens_pair = (pieces[0], pieces[1])
        mods = (pieces[2], pieces[3])
        valid_row = pieces[4]
        cotan_pair = (pieces[5], pieces[6])
        inputs = [tokens_pair[modality].astype(jnp.float32) for modality in range(2)]
        first_norm = [normalize(inputs[modality]) for modality in range(2)]
        normed_in = [(first_norm[modality][0] * (1.0 + mods[modality][1]) + mods[modality][0]).astype(jnp.bfloat16) for modality in range(2)]
        projected = [dense_product(normed_in[modality], inward[modality]).astype(jnp.bfloat16).reshape(lengths[modality], 3, D) for modality in range(2)]
        queries = jnp.concatenate([projected[0][:, 0], projected[1][:, 0]], axis=0).reshape(joint_len, H, HD)
        key_rows = jnp.concatenate([projected[0][:, 1], projected[1][:, 1]], axis=0).reshape(joint_len, H, HD)
        value_rows = jnp.concatenate([projected[0][:, 2], projected[1][:, 2]], axis=0).reshape(joint_len, H, HD)
        valid_keys = jnp.concatenate([jnp.ones((LI,), jnp.int32), valid_row]) > 0
        scores = jnp.einsum('qhd,khd->hqk', queries.astype(jnp.float32), key_rows.astype(jnp.float32)) * score_scale
        scores = jnp.where(valid_keys[None, None, :], scores, MASKED)
        highest = lax.optimization_barrier(jnp.max(scores, axis=2, keepdims=True))
        log_total = highest + jnp.log(lax.optimization_barrier(jnp.sum(jnp.exp(scores - highest), axis=2, keepdims=True)))
        softmax = jnp.exp(scores - log_total)
        weights = softmax.astype(jnp.bfloat16)
        attended = jnp.einsum('hqk,khd->qhd', weights.astype(jnp.float32), value_rows.astype(jnp.float32)).astype(jnp.bfloat16).reshape(joint_len, D)
        attn_parts = (attended[:LI], attended[LI:])
        branches = [dense_product(attn_parts[modality], outward[modality]) for modality in range(2)]
        middles = [inputs[modality] + mods[modality][2] * branches[modality] for modality in range(2)]
        second_norm = [normalize(middles[modality]) for modality in range(2)]
        mlp_in = [(second_norm[modality][0] * (1.0 + mods[modality][4]) + mods[modality][3]).astype(jnp.bfloat16) for modality in range(2)]
        pre_acts = [dense_product(mlp_in[modality], expand[modality]) for modality in range(2)]
        hiddens = [gelu_tanh(pre_acts[modality]).astype(jnp.bfloat16) for modality in range(2)]
        mlp_out = [dense_product(hiddens[modality], contract[modality]) for modality in range(2)]
        outputs = [(middles[modality] + mods[modality][5] * mlp_out[modality]).astype(jnp.bfloat16) for modality in range(2)]
        cotangents = [cotan_pair[modality].astype(jnp.float32) for modality in range(2)]
        gate_two = [lax.optimization_barrier(jnp.sum(cotangents[modality] * mlp_out[modality], axis=0)) for modality in range(2)]
        mlp_grad = [(mods[modality][5] * cotangents[modality]).astype(jnp.bfloat16) for modality in range(2)]
        grad_contract = [dense_product(hiddens[modality].T, mlp_grad[modality]) for modality in range(2)]
        dpre_act = [(dense_product(mlp_grad[modality], contract[modality].T) * gelu_slope(pre_acts[modality])).astype(jnp.bfloat16) for modality in range(2)]
        grad_expand = [dense_product(mlp_in[modality].T, dpre_act[modality]) for modality in range(2)]
        dmlp_in = [dense_product(dpre_act[modality], expand[modality].T) for modality in range(2)]
        scale_two = [lax.optimization_barrier(jnp.sum(dmlp_in[modality] * second_norm[modality][0], axis=0)) for modality in range(2)]
        shift_two = [lax.optimization_barrier(jnp.sum(dmlp_in[modality], axis=0)) for modality in range(2)]
        dmiddles = [cotangents[modality] + norm_back(dmlp_in[modality] * (1.0 + mods[modality][4]), second_norm[modality][0], second_norm[modality][1]) for modality in range(2)]
        gate_one = [lax.optimization_barrier(jnp.sum(dmiddles[modality] * branches[modality], axis=0)) for modality in range(2)]
        dbranch = [(mods[modality][2] * dmiddles[modality]).astype(jnp.bfloat16) for modality in range(2)]
        grad_outward = [dense_product(attn_parts[modality].T, dbranch[modality]) for modality in range(2)]
        dattn = [dense_product(dbranch[modality], outward[modality].T).astype(jnp.bfloat16) for modality in range(2)]
        dattn_joint = jnp.concatenate(dattn, axis=0).reshape(joint_len, H, HD)
        dvalue_rows = jnp.einsum('hqk,qhd->khd', weights.astype(jnp.float32), dattn_joint.astype(jnp.float32)).astype(jnp.bfloat16).reshape(joint_len, D)
        dprobs = jnp.einsum('qhd,khd->hqk', dattn_joint.astype(jnp.float32), value_rows.astype(jnp.float32))
        deltas = lax.optimization_barrier(jnp.sum(dattn_joint.astype(jnp.float32) * attended.reshape(joint_len, H, HD).astype(jnp.float32), axis=2))
        dscores = (softmax * (dprobs - deltas.T[:, :, None])).astype(jnp.bfloat16)
        dqueries = (jnp.einsum('hqk,khd->qhd', dscores.astype(jnp.float32), key_rows.astype(jnp.float32)) * score_scale).astype(jnp.bfloat16).reshape(joint_len, D)
        dkey_rows = (jnp.einsum('hqk,qhd->khd', dscores.astype(jnp.float32), queries.astype(jnp.float32)) * score_scale).astype(jnp.bfloat16).reshape(joint_len, D)
        bounds = ((0, LI), (LI, joint_len))
        grad_inward = []
        input_grads = []
        dmods = []
        for modality in range(2):
            lower, upper = bounds[modality]
            dprojected = jnp.stack([dqueries[lower:upper], dkey_rows[lower:upper], dvalue_rows[lower:upper]], axis=1).reshape(upper - lower, 3 * D)
            grad_inward.append(dense_product(normed_in[modality].T, dprojected))
            dnormed = dense_product(dprojected, inward[modality].T)
            scale_one = lax.optimization_barrier(jnp.sum(dnormed * first_norm[modality][0], axis=0))
            shift_one = lax.optimization_barrier(jnp.sum(dnormed, axis=0))
            input_grads.append(dmiddles[modality] + norm_back(dnormed * (1.0 + mods[modality][1]), first_norm[modality][0], first_norm[modality][1]))
            dmods.append(jnp.stack([shift_one, scale_one, gate_one[modality], shift_two[modality], scale_two[modality], gate_two[modality]], axis=0))
        updated = (carried[0] + grad_inward[0], carried[1] + grad_inward[1], carried[2] + grad_outward[0], carried[3] + grad_outward[1], carried[4] + grad_expand[0], carried[5] + grad_expand[1], carried[6] + grad_contract[0], carried[7] + grad_contract[1])
        return (updated, (outputs[0], outputs[1], input_grads[0], input_grads[1], dmods[0], dmods[1]))
    initial = (jnp.zeros((D, 3 * D), jnp.float32), jnp.zeros((D, 3 * D), jnp.float32), jnp.zeros((D, D), jnp.float32), jnp.zeros((D, D), jnp.float32), jnp.zeros((D, FF), jnp.float32), jnp.zeros((D, FF), jnp.float32), jnp.zeros((FF, D), jnp.float32), jnp.zeros((FF, D), jnp.float32))
    sequence_items = (image_tokens.reshape(SEQS, LI, D), text_tokens.reshape(SEQS, LT, D), modulations[0], modulations[1], text_valid, image_cotangent.reshape(SEQS, LI, D), text_cotangent.reshape(SEQS, LT, D))
    totals, stacked = lax.scan(one_sequence, initial, sequence_items)
    mod_grads = [dense_product(cond_silu.T, stacked[4 + modality].astype(jnp.bfloat16).reshape(SEQS, 6 * D)).reshape(D, 6, D) for modality in range(2)]
    return (stacked[0].reshape(SEQS * LI, D), stacked[1].reshape(SEQS * LT, D), stacked[2].reshape(SEQS * LI, D), stacked[3].reshape(SEQS * LT, D), mod_grads[0], mod_grads[1], totals[0].reshape(D, 3, D), totals[1].reshape(D, 3, D), totals[2], totals[3], totals[4], totals[5], totals[6], totals[7])
```

```python
import jax
import jax.numpy as jnp
from jax import lax
from jax.sharding import PartitionSpec as P


D = 1536
HD = 64


EPSILON = 1e-06
MASKED = -1e30
GELU_SCALE = 0.7978845608028654
GELU_CUBIC = 0.044715


def gelu_tanh(values):
    return (
        0.5
        * values
        * (1.0 + jnp.tanh(GELU_SCALE * (values + GELU_CUBIC * values * values * values)))
    )


def gelu_slope(values):
    tangent = jnp.tanh(GELU_SCALE * (values + GELU_CUBIC * values * values * values))
    return 0.5 * (1.0 + tangent) + 0.5 * values * (1.0 - tangent * tangent) * GELU_SCALE * (
        1.0 + 3.0 * GELU_CUBIC * values * values
    )


def dense_product(left, right):
    return jnp.dot(left, right, preferred_element_type=jnp.float32)


def ring_rows(rows):
    return [*range(0, rows, 2), *range(rows - 1, 0, -2)]


def ring_pairs(rows, step):
    order = ring_rows(rows)
    return [(order[i], order[(i + step) % rows]) for i in range(rows)]


def ring_place(rows):
    row = lax.axis_index("row")
    return jnp.where(row % 2 == 0, row // 2, rows - 1 - row // 2)


def ring_row_at(place, rows):
    place = place % rows
    return jnp.where(place < rows // 2, 2 * place, 2 * (rows - 1 - place) + 1)


def ring_gather(block, axis, sign):
    rows = lax.axis_size("row")
    place = ring_place(rows)
    length = block.shape[axis]
    shape = block.shape[:axis] + (rows * length,) + block.shape[axis + 1 :]

    def put(whole, piece, row):
        starts = [0] * block.ndim
        starts[axis] = row * length
        return lax.dynamic_update_slice(whole, piece, tuple(starts))

    whole = put(jnp.zeros(shape, block.dtype), block, lax.axis_index("row"))
    ahead = behind = block
    for hop in range(1, rows // 2 + 1):
        ahead = lax.ppermute(ahead, "row", ring_pairs(rows, sign))
        whole = put(whole, ahead, ring_row_at(place - sign * hop, rows))
        if hop < rows // 2:
            behind = lax.ppermute(behind, "row", ring_pairs(rows, -sign))
            whole = put(whole, behind, ring_row_at(place + sign * hop, rows))
    return whole


def ring_scatter(terms, axis, sign):
    rows = lax.axis_size("row")
    place = ring_place(rows)
    length = terms.shape[axis] // rows

    def block(at):
        return lax.dynamic_slice_in_dim(terms, ring_row_at(at, rows) * length, length, axis)

    def travel(way, hops):
        moving = lax.ppermute(block(place + way * hops), "row", ring_pairs(rows, way))
        for hop in range(hops - 1, 0, -1):
            moving = moving.astype(jnp.float32) + block(place + way * hop).astype(jnp.float32)
            moving = lax.ppermute(moving.astype(terms.dtype), "row", ring_pairs(rows, way))
        return moving.astype(jnp.float32)

    return (
        block(place).astype(jnp.float32)
        + travel(sign, rows // 2)
        + travel(-sign, rows // 2 - 1)
    )


def swap(values, bit):
    cols = lax.axis_size("col")
    return lax.ppermute(values, "col", [(c, c ^ bit) for c in range(cols)])


def col_bit(bit):
    return (lax.axis_index("col") // bit) % 2 == 1


def col_gather(values):
    cols = lax.axis_size("col")
    known = {0: values}
    bit = cols // 2
    while bit:
        known.update({k ^ bit: swap(v, bit) for k, v in list(known.items())})
        bit //= 2
    blocks = [known[k] for k in range(cols)]
    bit = 1
    while bit < cols:
        odd = col_bit(bit)
        blocks = [jnp.where(odd, blocks[k ^ bit], blocks[k]) for k in range(cols)]
        bit *= 2
    return jnp.concatenate(blocks, axis=-1)


def col_scatter(partial):
    cols = lax.axis_size("col")
    width = partial.shape[-1] // cols
    blocks = [partial[..., k * width : (k + 1) * width].astype(jnp.bfloat16) for k in range(cols)]
    bit = 1
    while len(blocks) > 1:
        odd = col_bit(bit)
        result = []
        for k in range(0, len(blocks), 2):
            sent = jnp.where(odd, blocks[k], blocks[k + 1]).astype(jnp.bfloat16)
            kept = jnp.where(odd, blocks[k + 1], blocks[k])
            result.append(kept.astype(jnp.float32) + swap(sent, bit).astype(jnp.float32))
        blocks = result
        bit *= 2
    return blocks[0]


def component(modulation, position):
    return modulation[:, None, position]


def moments(values):
    average = jnp.mean(values, axis=2, keepdims=True)
    squares = jnp.mean(values * values, axis=2, keepdims=True)
    return (average, lax.rsqrt(squares - average * average + EPSILON))


def item_scores(queries, key_rows, valid_keys):
    scores = jnp.einsum(
        "qd,kd->qk", queries, key_rows, preferred_element_type=jnp.float32
    ) * HD ** (-0.5)
    return jnp.where(valid_keys[None, :] > 0, scores, MASKED)


def attend_item(pieces):
    queries, key_rows, value_rows, valid_keys = pieces
    scores = item_scores(queries, key_rows, valid_keys)
    highest = jnp.max(scores, axis=1, keepdims=True)
    log_total = highest + jnp.log(jnp.sum(jnp.exp(scores - highest), axis=1, keepdims=True))
    weights = jnp.exp(scores - log_total).astype(jnp.bfloat16)
    output = jnp.einsum(
        "qk,kd->qd", weights, value_rows, preferred_element_type=jnp.float32
    ).astype(jnp.bfloat16)
    return (output, log_total[:, 0])


def attend_back(pieces):
    queries, key_rows, value_rows, valid_keys, output, log_total, upward = pieces
    scores = item_scores(queries, key_rows, valid_keys)
    softmax = jnp.exp(scores - log_total[:, None])
    dvalue_rows = jnp.einsum(
        "qk,qd->kd", softmax.astype(jnp.bfloat16), upward, preferred_element_type=jnp.float32
    ).astype(jnp.bfloat16)
    dprobs = jnp.einsum("qd,kd->qk", upward, value_rows, preferred_element_type=jnp.float32)
    deltas = jnp.sum(upward.astype(jnp.float32) * output.astype(jnp.float32), axis=1, keepdims=True)
    dscores = (softmax * (dprobs - deltas)).astype(jnp.bfloat16)
    dqueries = (
        jnp.einsum("qk,kd->qd", dscores, key_rows, preferred_element_type=jnp.float32)
        * HD ** (-0.5)
    ).astype(jnp.bfloat16)
    dkey_rows = (
        jnp.einsum("qk,qd->kd", dscores, queries, preferred_element_type=jnp.float32) * HD ** (-0.5)
    ).astype(jnp.bfloat16)
    return (dqueries, dkey_rows, dvalue_rows)


def to_items(former, latter, head_count):
    joined = jnp.concatenate([former, latter], axis=1)
    seq_count, length, local_width = joined.shape
    head_size = local_width // head_count
    return (
        joined.reshape(seq_count, length, head_count, head_size)
        .transpose(0, 2, 1, 3)
        .reshape(seq_count * head_count, length, head_size)
    )


def from_items(pieces, seq_count, head_count, boundary):
    length, head_size = (pieces.shape[1], pieces.shape[2])
    joined = (
        pieces.reshape(seq_count, head_count, length, head_size)
        .transpose(0, 2, 1, 3)
        .reshape(seq_count, length, head_count * head_size)
    )
    return (joined[:, :boundary], joined[:, boundary:])


def local(
    image_tokens,
    text_tokens,
    conditioning,
    text_valid,
    image_modulation,
    text_modulation,
    image_inward,
    text_inward,
    image_outward,
    text_outward,
    image_expand,
    text_expand,
    image_contract,
    text_contract,
    image_cotangent,
    text_cotangent,
):
    both = range(2)
    seq_count = conditioning.shape[0]
    local_width = image_tokens.shape[1]
    head_count = local_width // HD
    lengths = (image_tokens.shape[0] // seq_count, text_tokens.shape[0] // seq_count)
    row = lax.axis_index("row")
    col = lax.axis_index("col")
    signs = (1, -1)

    def by_sequence(values, modality):
        return values.reshape(seq_count, lengths[modality], -1)

    tokens = [by_sequence(v, m) for m, v in enumerate((image_tokens, text_tokens))]
    cotan = [by_sequence(v, m) for m, v in enumerate((image_cotangent, text_cotangent))]
    inputs = [tokens[m].astype(jnp.float32) for m in both]
    cotangents = [cotan[m].astype(jnp.float32) for m in both]

    cond_silu = jax.nn.silu(conditioning.astype(jnp.float32)).astype(jnp.bfloat16)
    cond_all = lax.all_gather(cond_silu, "row", axis=0, tiled=True)
    mod_rows = image_modulation.shape[0]
    cond_mine = lax.dynamic_slice_in_dim(cond_all, row * mod_rows, mod_rows, 1)
    mod_terms = jnp.stack(
        [
            jnp.einsum("sd,dkf->skf", cond_mine, table, preferred_element_type=jnp.float32)
            for table in (image_modulation, text_modulation)
        ],
        axis=1,
    )
    mod_local = lax.psum_scatter(mod_terms, "row", scatter_dimension=0, tiled=True)
    mod_full = lax.all_gather(mod_local, "col", axis=3, tiled=True)
    mods = [mod_local[:, m] for m in both]
    wide_mods = [mod_full[:, m] for m in both]

    inward = [
        ring_gather(w.transpose(1, 0, 2), 1, signs[m])
        for m, w in enumerate((image_inward, text_inward))
    ]
    outward = [ring_gather(w.T, 0, signs[m]) for m, w in enumerate((image_outward, text_outward))]
    expand = [ring_gather(w, 0, signs[m]) for m, w in enumerate((image_expand, text_expand))]
    contract = [
        ring_gather(w.T, 0, signs[m]) for m, w in enumerate((image_contract, text_contract))
    ]

    wide_tokens = [col_gather(tokens[m]) for m in both]
    wide_cotan = [col_gather(cotan[m]) for m in both]

    first = [moments(wide_tokens[m].astype(jnp.float32)) for m in both]
    act = [
        (
            (wide_tokens[m].astype(jnp.float32) - first[m][0])
            * first[m][1]
            * (1.0 + component(wide_mods[m], 1))
            + component(wide_mods[m], 0)
        ).astype(jnp.bfloat16)
        for m in both
    ]
    projected = [
        jnp.einsum("std,pdf->pstf", act[m], inward[m], preferred_element_type=jnp.float32).astype(
            jnp.bfloat16
        )
        for m in both
    ]
    valid_joint = jnp.concatenate(
        [jnp.ones((seq_count, lengths[0]), jnp.int32), text_valid], axis=1
    )
    valid_items = jnp.broadcast_to(
        valid_joint[:, None, :], (seq_count, head_count, valid_joint.shape[1])
    ).reshape(seq_count * head_count, -1)
    query_items = to_items(projected[0][0], projected[1][0], head_count)
    key_items = to_items(projected[0][1], projected[1][1], head_count)
    value_items = to_items(projected[0][2], projected[1][2], head_count)
    attended, log_totals = lax.map(attend_item, (query_items, key_items, value_items, valid_items))
    attn = from_items(attended, seq_count, head_count, lengths[0])

    branch = [
        col_scatter(jnp.einsum("stf,df->std", attn[m], outward[m], preferred_element_type=jnp.float32))
        for m in both
    ]
    wide_branch = [col_gather(branch[m].astype(jnp.bfloat16)).astype(jnp.float32) for m in both]
    middle = [inputs[m] + component(mods[m], 2) * branch[m] for m in both]
    wide_middle = [
        wide_tokens[m].astype(jnp.float32) + component(wide_mods[m], 2) * wide_branch[m]
        for m in both
    ]
    second = [moments(wide_middle[m]) for m in both]
    wide_normed = [(wide_middle[m] - second[m][0]) * second[m][1] for m in both]
    mlp_in = [
        (wide_normed[m] * (1.0 + component(wide_mods[m], 4)) + component(wide_mods[m], 3)).astype(
            jnp.bfloat16
        )
        for m in both
    ]
    pre = [
        jnp.einsum("std,dh->sth", mlp_in[m], expand[m], preferred_element_type=jnp.float32)
        for m in both
    ]
    hidden = [gelu_tanh(pre[m]).astype(jnp.bfloat16) for m in both]
    mlp_out = [
        col_scatter(
            jnp.einsum("sth,dh->std", hidden[m], contract[m], preferred_element_type=jnp.float32)
        )
        for m in both
    ]
    outputs = [
        (middle[m] + component(mods[m], 5) * mlp_out[m]).astype(jnp.bfloat16).reshape(-1, local_width)
        for m in both
    ]

    gate_two = [jnp.sum(cotangents[m] * mlp_out[m], axis=1) for m in both]
    mlp_grad = [
        (component(wide_mods[m], 5) * wide_cotan[m].astype(jnp.float32)).astype(jnp.bfloat16)
        for m in both
    ]
    contract_terms = [
        jnp.einsum("std,sth->dh", mlp_grad[m], hidden[m], preferred_element_type=jnp.float32).astype(
            jnp.bfloat16
        )
        for m in both
    ]
    dpre = [
        (
            jnp.einsum("std,dh->sth", mlp_grad[m], contract[m], preferred_element_type=jnp.float32)
            * gelu_slope(pre[m])
        ).astype(jnp.bfloat16)
        for m in both
    ]
    expand_terms = [
        jnp.einsum("std,sth->dh", mlp_in[m], dpre[m], preferred_element_type=jnp.float32).astype(
            jnp.bfloat16
        )
        for m in both
    ]
    dmlp_in = [
        col_scatter(
            jnp.einsum("sth,dh->std", dpre[m], expand[m], preferred_element_type=jnp.float32)
        )
        for m in both
    ]
    wide_dmlp_in = [col_gather(dmlp_in[m].astype(jnp.bfloat16)).astype(jnp.float32) for m in both]
    normed_two = [(middle[m] - second[m][0]) * second[m][1] for m in both]
    scale_two = [jnp.sum(dmlp_in[m] * normed_two[m], axis=1) for m in both]
    shift_two = [jnp.sum(dmlp_in[m], axis=1) for m in both]
    dmiddle = []
    dbranch = []
    for m in both:
        upward = wide_dmlp_in[m] * (1.0 + component(wide_mods[m], 4))
        mean_up = jnp.mean(upward, axis=2, keepdims=True)
        mean_prod = jnp.mean(upward * wide_normed[m], axis=2, keepdims=True)
        inverse = second[m][1]
        wide_dmiddle = wide_cotan[m].astype(jnp.float32) + inverse * (
            upward - mean_up - wide_normed[m] * mean_prod
        )
        dbranch.append((component(wide_mods[m], 2) * wide_dmiddle).astype(jnp.bfloat16))
        dmiddle.append(
            cotangents[m]
            + inverse
            * (
                dmlp_in[m] * (1.0 + component(mods[m], 4))
                - mean_up
                - normed_two[m] * mean_prod
            )
        )
    gate_one = [jnp.sum(dmiddle[m] * branch[m], axis=1) for m in both]
    outward_terms = [
        jnp.einsum("std,stf->df", dbranch[m], attn[m], preferred_element_type=jnp.float32).astype(
            jnp.bfloat16
        )
        for m in both
    ]
    dattn = [
        jnp.einsum("std,df->stf", dbranch[m], outward[m], preferred_element_type=jnp.float32).astype(
            jnp.bfloat16
        )
        for m in both
    ]
    dattn_items = to_items(dattn[0], dattn[1], head_count)
    ditems = lax.map(
        attend_back,
        (query_items, key_items, value_items, valid_items, attended, log_totals, dattn_items),
    )
    dparts = [from_items(d, seq_count, head_count, lengths[0]) for d in ditems]
    dprojected = [jnp.stack([dparts[p][m] for p in range(3)]) for m in both]
    inward_terms = [
        jnp.einsum("std,pstf->pdf", act[m], dprojected[m], preferred_element_type=jnp.float32).astype(
            jnp.bfloat16
        )
        for m in both
    ]
    dact = [
        col_scatter(
            jnp.einsum("pstf,pdf->std", dprojected[m], inward[m], preferred_element_type=jnp.float32)
        )
        for m in both
    ]
    normed_one = [(inputs[m] - first[m][0]) * first[m][1] for m in both]
    scale_one = [jnp.sum(dact[m] * normed_one[m], axis=1) for m in both]
    shift_one = [jnp.sum(dact[m], axis=1) for m in both]
    upward = [dact[m] * (1.0 + component(mods[m], 1)) for m in both]
    totals = lax.psum(
        [(jnp.sum(upward[m], axis=2), jnp.sum(upward[m] * normed_one[m], axis=2)) for m in both],
        "col",
    )
    input_grads = [
        (
            dmiddle[m]
            + first[m][1]
            * (
                upward[m]
                - (totals[m][0] / D)[:, :, None]
                - normed_one[m] * (totals[m][1] / D)[:, :, None]
            )
        ).reshape(-1, local_width)
        for m in both
    ]
    dmods = jnp.stack(
        [
            jnp.stack(
                [shift_one[m], scale_one[m], gate_one[m], shift_two[m], scale_two[m], gate_two[m]],
                axis=1,
            )
            for m in both
        ],
        axis=1,
    ).astype(jnp.bfloat16)
    dmods_all = lax.all_gather(dmods, "row", axis=0, tiled=True)
    mod_grads = [
        jnp.einsum("sd,skf->dkf", cond_mine, dmods_all[:, m], preferred_element_type=jnp.float32)
        for m in both
    ]
    contract_grads = [ring_scatter(contract_terms[m], 0, signs[m]).T for m in both]
    expand_grads = [ring_scatter(expand_terms[m], 0, signs[m]) for m in both]
    outward_grads = [ring_scatter(outward_terms[m], 0, signs[m]).T for m in both]
    inward_grads = [ring_scatter(inward_terms[m], 1, signs[m]).transpose(1, 0, 2) for m in both]
    return (
        *outputs,
        *input_grads,
        *mod_grads,
        *inward_grads,
        *outward_grads,
        *expand_grads,
        *contract_grads,
    )


def solution(mesh):
    placed = (
        P("row", "col"),
        P("row", "col"),
        P("row", None),
        P("row", None),
        P("row", None, "col"),
        P("row", None, "col"),
        P("row", None, "col"),
        P("row", None, "col"),
        P("col", "row"),
        P("col", "row"),
        P("row", "col"),
        P("row", "col"),
        P("col", "row"),
        P("col", "row"),
        P("row", "col"),
        P("row", "col"),
    )
    return jax.shard_map(
        local,
        mesh=mesh,
        in_specs=placed,
        out_specs=(
            P("row", "col"),
            P("row", "col"),
            P("row", "col"),
            P("row", "col"),
            P("row", None, "col"),
            P("row", None, "col"),
            P("row", None, "col"),
            P("row", None, "col"),
            P("col", "row"),
            P("col", "row"),
            P("row", "col"),
            P("row", "col"),
            P("col", "row"),
            P("col", "row"),
        ),
        check_vma=False,
    )
```

```python
import functools

import jax
import jax.numpy as jnp
from jax import lax
from jax.experimental import pallas as pl
from jax.experimental.pallas import tpu as pltpu
from jax.sharding import PartitionSpec as P


HD = 64


TILE = 256
EPSILON = 1e-06
MASKED = -1e30
GELU_SCALE = 0.7978845608028654
GELU_CUBIC = 0.044715


def gelu_tanh(values):
    return (
        0.5
        * values
        * (1.0 + jnp.tanh(GELU_SCALE * (values + GELU_CUBIC * values * values * values)))
    )


def gelu_slope(values):
    tangent = jnp.tanh(GELU_SCALE * (values + GELU_CUBIC * values * values * values))
    return 0.5 * (1.0 + tangent) + 0.5 * values * (1.0 - tangent * tangent) * GELU_SCALE * (
        1.0 + 3.0 * GELU_CUBIC * values * values
    )


class Flow:
    def __init__(self, rounds=None):
        self.waiting = []
        self.flying = []
        self.rounds = None
        self.results = []
        if rounds is not None:
            self.follow(rounds)

    def follow(self, rounds):
        self.rounds = rounds
        self.flying = next(rounds)

    def queue(self, make, operands):
        self.waiting.append((make, operands))
        return self

    def begin(self):
        if self.rounds is None and self.waiting:
            make, operands = self.waiting.pop(0)
            self.follow(make(operands))

    def land(self, flying, coming):
        if self.rounds is None:
            return
        try:
            self.flying = self.rounds.send(flying)
        except StopIteration as stop:
            self.results.append(stop.value)
            self.rounds, self.flying = None, []
            if self.waiting:
                make, _ = self.waiting.pop(0)
                self.follow(make(coming))


def tick(flows, values=()):
    flows = [f for f in flows if f.rounds is not None]
    coming = [f.waiting[0][1] if f.waiting else [] for f in flows]
    flying, coming, values = lax.optimization_barrier(([f.flying for f in flows], coming, values))
    for flow, landed, operands in zip(flows, flying, coming):
        flow.land(landed, operands)
    return values


def finish(flow):
    while flow.rounds is not None:
        tick([flow])
    return flow.results[-1]


def settle(flow, rings):
    turn = 0
    while flow.rounds is not None:
        tick([flow, rings[turn % len(rings)]])
        turn += 1
    return flow.results[-1]


def ring_rows(rows):
    return [*range(0, rows, 2), *range(rows - 1, 0, -2)]


def ring_send(values, way):
    rows = lax.axis_size("row")
    order = ring_rows(rows)
    return lax.ppermute(
        values, "row", [(order[i], order[(i + way) % rows]) for i in range(rows)]
    )


def ring_place(rows):
    row = lax.axis_index("row")
    return jnp.where(row % 2 == 0, row // 2, rows - 1 - row // 2)


def ring_row_at(place, rows):
    place = place % rows
    return jnp.where(place < rows // 2, 2 * place, 2 * (rows - 1 - place) + 1)


def gather_rounds(block, axis, way):
    rows = lax.axis_size("row")
    place = ring_place(rows)
    half = rows // 2
    length = block.shape[axis]
    shape = block.shape[:axis] + (rows * length,) + block.shape[axis + 1 :]

    def put(whole, piece, row):
        return lax.dynamic_update_slice_in_dim(whole, piece, row * length, axis)

    ahead, behind = ring_send(block, way), ring_send(block, -way)
    whole = put(jnp.zeros(shape, block.dtype), block, lax.axis_index("row"))
    for hop in range(1, half + 1):
        landed = yield [ahead, behind] if hop < half else [ahead]
        if hop < half:
            ahead = ring_send(landed[0], way)
        if hop + 1 < half:
            behind = ring_send(landed[1], -way)
        whole = put(whole, landed[0], ring_row_at(place + -way * hop, rows))
        if hop < half:
            whole = put(whole, landed[1], ring_row_at(place + way * hop, rows))
    return whole


def scatter_rounds(terms, axis, way):
    rows = lax.axis_size("row")
    place = ring_place(rows)
    half = rows // 2
    length = terms[0].shape[axis] // rows

    def block(at):
        start = ring_row_at(at, rows) * length
        return jnp.stack([lax.dynamic_slice_in_dim(t, start, length, axis) for t in terms])

    def joined(moving, at):
        total = moving.astype(jnp.float32) + block(at).astype(jnp.float32)
        return total.astype(jnp.bfloat16)

    ahead = ring_send(block(place + way * half), way)
    behind = ring_send(block(place - way * (half - 1)), -way)
    for hop in range(1, half + 1):
        landed = yield [ahead, behind] if hop < half else [ahead]
        if hop < half:
            ahead = ring_send(joined(landed[0], place + way * (half - hop)), way)
            behind = landed[1]
        if hop + 1 < half:
            behind = ring_send(joined(behind, place - way * (half - 1 - hop)), -way)
    return (
        block(place).astype(jnp.float32)
        + landed[0].astype(jnp.float32)
        + behind.astype(jnp.float32)
    )


def row_swap(values, bit):
    rows = lax.axis_size("row")
    return lax.ppermute(values, "row", [(r, r ^ bit) for r in range(rows)])


def row_gather_rounds(values):
    known = values[None]
    bit = 1
    while bit < lax.axis_size("row"):
        (landed,) = yield [row_swap(known, bit)]
        known = jnp.concatenate([known, landed])
        bit *= 2
    return known


def row_scatter_rounds(terms):
    bit = lax.axis_size("row") // 2
    while bit:
        (landed,) = yield [row_swap(terms[bit:], bit)]
        terms = terms[:bit] + landed
        bit //= 2
    return terms[0]


def swap(values, bit):
    cols = lax.axis_size("col")
    return lax.ppermute(values, "col", [(c, c ^ bit) for c in range(cols)])


def col_bit(bit):
    return (lax.axis_index("col") // bit) % 2 == 1


def col_gather_rounds(parts):
    cols = lax.axis_size("col")
    known = [{0: p} for p in parts]
    bit = cols // 2
    while bit:
        held = [list(k) for k in known]
        landed = yield [swap(k[n], bit) for k, names in zip(known, held) for n in names]
        for k, names in zip(known, held):
            for name in names:
                k[name ^ bit] = landed.pop(0)
        bit //= 2
    wholes = []
    for k in known:
        blocks = [k[n] for n in range(cols)]
        bit = 1
        while bit < cols:
            odd = col_bit(bit)
            blocks = [jnp.where(odd, blocks[n ^ bit], blocks[n]) for n in range(cols)]
            bit *= 2
        wholes.append(jnp.concatenate(blocks, axis=-1))
    return wholes


def col_scatter_rounds(partials):
    cols = lax.axis_size("col")
    blocks = [jnp.split(p.astype(jnp.bfloat16), cols, axis=-1) for p in partials]
    bit = 1
    while len(blocks[0]) > 1:
        odd = col_bit(bit)
        sent = []
        kept = []
        for b in blocks:
            for k in range(0, len(b), 2):
                sent.append(jnp.where(odd, b[k], b[k + 1]).astype(jnp.bfloat16))
                kept.append(jnp.where(odd, b[k + 1], b[k]).astype(jnp.float32))
        landed = yield [swap(v, bit) for v in sent]
        totals = [a + b.astype(jnp.float32) for a, b in zip(kept, landed)]
        count = len(blocks[0]) // 2
        blocks = [totals[i : i + count] for i in range(0, len(totals), count)]
        bit *= 2
    return [b[0] for b in blocks]


def col_sum_rounds(values):
    bit = 1
    while bit < lax.axis_size("col"):
        (landed,) = yield [swap(values, bit)]
        values = values + landed
        bit *= 2
    return values


def component(modulation, position):
    return modulation[:, None, position]


def moments(values):
    average = jnp.mean(values, axis=2, keepdims=True)
    squares = jnp.mean(values * values, axis=2, keepdims=True)
    return (average, lax.rsqrt(squares - average * average + EPSILON))


def product(spec, left, right):
    return jnp.einsum(spec, left, right, preferred_element_type=jnp.float32)


def head_lanes(values, head):
    lane = lax.broadcasted_iota(jnp.int32, values.shape, 1)
    return jnp.where(lane // HD == head, values, jnp.zeros_like(values))


def lanes_product(left, right):
    return lax.dot_general(
        left, right, (((1,), (1,)), ((), ())), preferred_element_type=jnp.float32
    )


def attend_kernel(bias_ref, query_ref, key_ref, value_ref, out_ref, log_ref, *, tile):
    keys = key_ref[0]
    value_t = value_ref[0].T
    bias = bias_ref[0]
    heads = keys.shape[1] // HD

    def step(at, carry):
        rows = pl.ds(pl.multiple_of(at * tile, tile), tile)
        queries = query_ref[0, rows, :] * jnp.bfloat16(HD ** (-0.5))
        outs = []
        for head in range(heads):
            scores = lanes_product(keys, head_lanes(queries, head)) + bias
            highest = jnp.max(scores, axis=0, keepdims=True)
            powers = jnp.exp(scores - highest)
            total = jnp.sum(powers, axis=0, keepdims=True)
            probs = (powers * (1.0 / total)).astype(jnp.bfloat16)
            outs.append(
                jnp.dot(
                    value_t[head * HD : (head + 1) * HD],
                    probs,
                    preferred_element_type=jnp.float32,
                )
            )
            log_ref[0, 0, pl.ds(head, 1), rows] = highest + jnp.log(total)
        out_ref[0, rows, :] = jnp.concatenate(outs, axis=0).T.astype(jnp.bfloat16)
        return carry

    lax.fori_loop(0, query_ref.shape[1] // tile, step, 0)


def attend_back_kernel(
    bias_ref,
    query_ref,
    key_ref,
    value_ref,
    out_ref,
    log_ref,
    up_ref,
    dquery_ref,
    dkey_ref,
    dvalue_ref,
    dkey_sum,
    dvalue_sum,
    *,
    tile,
):
    keys = key_ref[0]
    values = value_ref[0]
    key_t = keys.T
    bias = bias_ref[0]
    heads = keys.shape[1] // HD
    dkey_sum[...] = jnp.zeros_like(dkey_sum)
    dvalue_sum[...] = jnp.zeros_like(dvalue_sum)

    def step(at, carry):
        rows = pl.ds(pl.multiple_of(at * tile, tile), tile)
        queries = query_ref[0, rows, :] * jnp.bfloat16(HD ** (-0.5))
        upward = up_ref[0, rows, :]
        products = (upward.astype(jnp.float32) * out_ref[0, rows, :].astype(jnp.float32)).T
        dqueries = []
        for head in range(heads):
            span = slice(head * HD, (head + 1) * HD)
            my_queries = head_lanes(queries, head)
            my_upward = head_lanes(upward, head)
            scores = lanes_product(keys, my_queries) + bias
            softmax = jnp.exp(scores - log_ref[0, 0, pl.ds(head, 1), rows])
            dvalue_sum[...] += jnp.dot(
                softmax.astype(jnp.bfloat16), my_upward, preferred_element_type=jnp.float32
            )
            deltas = jnp.sum(products[span], axis=0, keepdims=True)
            dscores = (softmax * (lanes_product(values, my_upward) - deltas)).astype(jnp.bfloat16)
            dkey_sum[...] += jnp.dot(dscores, my_queries, preferred_element_type=jnp.float32)
            dqueries.append(jnp.dot(key_t[span], dscores, preferred_element_type=jnp.float32))
        dquery = jnp.concatenate(dqueries, axis=0).T * HD ** (-0.5)
        dquery_ref[0, rows, :] = dquery.astype(jnp.bfloat16)
        return carry

    lax.fori_loop(0, query_ref.shape[1] // tile, step, 0)
    dkey_ref[0] = dkey_sum[...].astype(jnp.bfloat16)
    dvalue_ref[0] = dvalue_sum[...].astype(jnp.bfloat16)


def pair_specs(joint, first_pair):
    seq_count, length, width = joint.shape
    pairs = width // (3 * 2 * HD)

    def pair(offset):
        return pl.BlockSpec((1, length, 2 * HD), lambda s: (s, 0, offset))

    parts = [pair(first_pair + part * pairs) for part in range(3)]
    bias = pl.BlockSpec((1, length, 1), lambda s: (s, 0, 0))
    logs = pl.BlockSpec((1, 1, 2, length), lambda s: (s, 0, 0, 0))
    cost = pl.CostEstimate(
        flops=8 * seq_count * length * length * 2 * HD,
        transcendentals=seq_count * 2 * length * length,
        bytes_accessed=8 * seq_count * length * 2 * HD,
    )
    return pair, parts, bias, logs, cost


def attend_pair(bias, joint, which, tile=TILE):
    seq_count, length, _ = joint.shape
    pair, parts, bias_spec, logs, cost = pair_specs(joint, which)
    return pl.pallas_call(
        functools.partial(attend_kernel, tile=tile),
        grid=(seq_count,),
        in_specs=[bias_spec, *parts],
        out_specs=[pair(0), logs],
        out_shape=[
            jax.ShapeDtypeStruct((seq_count, length, 2 * HD), jnp.bfloat16),
            jax.ShapeDtypeStruct((seq_count, 1, 2, length), jnp.float32),
        ],
        cost_estimate=cost,
        name="attend_pair",
    )(bias, joint, joint, joint)


def attend_back_pair(bias, joint, out, logs, upward, which, tile=TILE):
    seq_count, length, _ = joint.shape
    pair, parts, bias_spec, log_spec, cost = pair_specs(joint, which)
    return pl.pallas_call(
        functools.partial(attend_back_kernel, tile=tile),
        grid=(seq_count,),
        in_specs=[bias_spec, *parts, pair(0), log_spec, pair(which)],
        out_specs=[pair(0)] * 3,
        out_shape=[jax.ShapeDtypeStruct((seq_count, length, 2 * HD), jnp.bfloat16)] * 3,
        scratch_shapes=[pltpu.VMEM((length, 2 * HD), jnp.float32)] * 2,
        cost_estimate=cost,
        name="attend_back_pair",
    )(bias, joint, joint, joint, out, logs, upward)


def local(
    image_tokens,
    text_tokens,
    conditioning,
    text_valid,
    image_modulation,
    text_modulation,
    image_inward,
    text_inward,
    image_outward,
    text_outward,
    image_expand,
    text_expand,
    image_contract,
    text_contract,
    image_cotangent,
    text_cotangent,
):
    both = range(2)
    seq_count = conditioning.shape[0]
    local_width = image_tokens.shape[1]
    features = local_width * lax.axis_size("col")
    lengths = (image_tokens.shape[0] // seq_count, text_tokens.shape[0] // seq_count)
    joint_length = -(-sum(lengths) // TILE) * TILE
    padded = (lengths[0], joint_length - lengths[0])
    pairs = local_width // (2 * HD)
    row = lax.axis_index("row")
    float32 = jnp.float32
    bfloat16 = jnp.bfloat16

    def by_sequence(values, modality):
        return values.reshape(seq_count, lengths[modality], -1)

    def pad_rows(values, modality):
        rest = padded[modality] - lengths[modality]
        return jnp.pad(values, ((0, 0), (0, rest), (0, 0)))

    tokens = [by_sequence(v, m) for m, v in enumerate((image_tokens, text_tokens))]
    cotan = [by_sequence(v, m) for m, v in enumerate((image_cotangent, text_cotangent))]
    inputs = [tokens[m].astype(float32) for m in both]
    cotangents = [cotan[m].astype(float32) for m in both]

    def blocks_of(m):
        return [
            (image_inward, text_inward)[m].reshape(-1, 3 * local_width),
            (image_outward, text_outward)[m].T,
            (image_expand, text_expand)[m],
            (image_contract, text_contract)[m].T,
        ]

    rings = [Flow(), Flow()]
    for m in both:
        for block in blocks_of(m):
            rings[m].queue(functools.partial(gather_rounds, axis=0, way=(1, -1)[m]), block)
        rings[m].begin()
    one, two = ([r] for r in rings)

    cond_silu = jax.nn.silu(conditioning.astype(float32)).astype(bfloat16)
    cond_flow = Flow(row_gather_rounds(cond_silu))
    token_flow = Flow(col_gather_rounds(tokens))
    cond_all = settle(cond_flow, rings)
    mod_rows = image_modulation.shape[0]
    cond_mine = lax.dynamic_slice_in_dim(cond_all, row * mod_rows, mod_rows, 2)
    mod_terms = jnp.stack(
        [product("rsd,dkf->rskf", cond_mine, t) for t in (image_modulation, text_modulation)],
        axis=2,
    )
    mod_local = settle(Flow(row_scatter_rounds(mod_terms)), rings[::-1])
    mods = [mod_local[:, m] for m in both]
    wide_flow = Flow(col_gather_rounds([mod_local]))
    tick([token_flow])
    wide_tokens = finish(token_flow)
    first = [moments(wide_tokens[m].astype(float32)) for m in both]
    tick([wide_flow])
    (mod_full,) = finish(wide_flow)
    wide_mods = [mod_full[:, m] for m in both]
    cotan_flow = Flow(col_gather_rounds(cotan))
    while min(len(r.results) for r in rings) < 1:
        for ring in rings:
            if len(ring.results) < 1:
                tick([ring])
    inward = [r.results[0] for r in rings]

    act = [
        pad_rows(
            (
                (wide_tokens[m].astype(float32) - first[m][0])
                * first[m][1]
                * (1.0 + component(wide_mods[m], 1))
                + component(wide_mods[m], 0)
            ).astype(bfloat16),
            m,
        )
        for m in both
    ]
    act = tick(rings, act)
    projected = [product("std,df->stf", act[m], inward[m]).astype(bfloat16) for m in both]
    projected = tick(rings, projected)
    joint = jnp.concatenate(projected, axis=1)
    valid = jnp.concatenate(
        [
            jnp.ones((seq_count, lengths[0]), jnp.int32),
            text_valid,
            jnp.zeros((seq_count, padded[1] - lengths[1]), jnp.int32),
        ],
        axis=1,
    )
    bias = jnp.where(valid > 0, 0.0, MASKED)[:, :, None]
    joint, bias = tick(rings, (joint, bias))
    while min(len(r.results) for r in rings) < 2:
        tick(rings)
    attended = []
    for p in range(pairs):
        attended.append(attend_pair(bias, joint, p))
        joint, attended[p] = tick([rings[p % 2]], (joint, attended[p]))
    outward = [r.results[1] for r in rings]
    joint_attn = jnp.concatenate([a[0] for a in attended], axis=2)
    attn = [joint_attn[:, : padded[0]], joint_attn[:, padded[0] :]]

    branch_flow = Flow(
        col_scatter_rounds(
            [product("stf,df->std", attn[m], outward[m])[:, : lengths[m]] for m in both]
        )
    )
    tick([branch_flow])
    tick(two)
    tick([branch_flow])
    branch = finish(branch_flow)
    wide_flow = Flow(col_gather_rounds([branch[m].astype(bfloat16) for m in both]))
    wide_cotan = finish(cotan_flow)
    mlp_grad = [
        (component(wide_mods[m], 5) * wide_cotan[m].astype(float32)).astype(bfloat16)
        for m in both
    ]
    mlp_grad = tick(one, mlp_grad)
    tick([wide_flow])
    tick(two)
    wide_branch = finish(wide_flow)
    middle = [inputs[m] + component(mods[m], 2) * branch[m] for m in both]
    wide_middle = [
        wide_tokens[m].astype(float32)
        + component(wide_mods[m], 2) * wide_branch[m].astype(float32)
        for m in both
    ]
    second = [moments(wide_middle[m]) for m in both]
    wide_normed = [(wide_middle[m] - second[m][0]) * second[m][1] for m in both]
    mlp_in = [
        (wide_normed[m] * (1.0 + component(wide_mods[m], 4)) + component(wide_mods[m], 3)).astype(
            bfloat16
        )
        for m in both
    ]
    mlp_in = tick(one, mlp_in)
    while min(len(r.results) for r in rings) < 3:
        for ring in rings:
            if len(ring.results) < 3:
                tick([ring])
    expand = [r.results[2] for r in rings]

    pre = [product("std,dh->sth", mlp_in[m], expand[m]) for m in both]
    hidden = [gelu_tanh(pre[m]).astype(bfloat16) for m in both]
    pre, hidden = tick(one, (pre, hidden))
    contract_terms = []
    for m in both:
        contract_terms.append(product("std,sth->dh", mlp_grad[m], hidden[m]).astype(bfloat16))
        contract_terms = tick([rings[1 - m]], contract_terms)
    while min(len(r.results) for r in rings) < 4:
        for ring in rings[::-1]:
            tick([ring])
    contract = [r.results[3] for r in rings]

    def add_terms(terms, way):
        return functools.partial(scatter_rounds, axis=0, way=way), terms

    sums = [Flow(), Flow()]
    one, two = ([f] for f in sums)
    sums[0].queue(*add_terms(contract_terms, 1)).begin()
    dpre = [
        (product("std,dh->sth", mlp_grad[m], contract[m]) * gelu_slope(pre[m])).astype(bfloat16)
        for m in both
    ]
    dpre = tick(one, dpre)
    dmlp_flow = Flow(
        col_scatter_rounds([product("sth,dh->std", dpre[m], expand[m]) for m in both])
    )
    dpre = tick([dmlp_flow], dpre)
    expand_terms = [product("std,sth->dh", mlp_in[m], dpre[m]).astype(bfloat16) for m in both]
    sums[1].queue(*add_terms(expand_terms, -1)).begin()
    tick([dmlp_flow])
    dmlp_in = finish(dmlp_flow)
    wide_flow = Flow(col_gather_rounds([dmlp_in[m].astype(bfloat16) for m in both]))
    mlp_terms = [product("sth,dh->std", hidden[m], contract[m]) for m in both]
    mlp_terms = tick(one, mlp_terms)
    tick([wide_flow])
    tick([wide_flow])
    wide_dmlp_in = finish(wide_flow)
    mlp_flow = Flow(col_scatter_rounds(mlp_terms))
    normed_two = [(middle[m] - second[m][0]) * second[m][1] for m in both]
    dmiddle = []
    dbranch = []
    for m in both:
        upward = wide_dmlp_in[m].astype(float32) * (1.0 + component(wide_mods[m], 4))
        mean_up = jnp.mean(upward, axis=2, keepdims=True)
        mean_prod = jnp.mean(upward * wide_normed[m], axis=2, keepdims=True)
        inverse = second[m][1]
        wide_dmiddle = wide_cotan[m].astype(float32) + inverse * (
            upward - mean_up - wide_normed[m] * mean_prod
        )
        dbranch.append(
            pad_rows((component(wide_mods[m], 2) * wide_dmiddle).astype(bfloat16), m)
        )
        dmiddle.append(
            cotangents[m]
            + inverse
            * (dmlp_in[m] * (1.0 + component(mods[m], 4)) - mean_up - normed_two[m] * mean_prod)
        )
    dbranch = tick(two, dbranch)
    joint_dattn = jnp.concatenate(
        [product("std,df->stf", dbranch[m], outward[m]).astype(bfloat16) for m in both], axis=1
    )
    outward_terms = [
        product("std,stf->df", dbranch[m], attn[m]).astype(bfloat16) for m in both
    ]
    joint_dattn, outward_terms = tick(one, (joint_dattn, outward_terms))
    sums[0].queue(*add_terms(outward_terms, 1))
    sums[0].begin()
    backs = []
    for p in range(pairs):
        backs.append(attend_back_pair(bias, joint, *attended[p], joint_dattn, p))
        joint_dattn, backs[p] = tick(
            [sums[1 - p % 2], mlp_flow] if p < 2 else [sums[1 - p % 2]], (joint_dattn, backs[p])
        )
    mlp_out = finish(mlp_flow)
    joint_back = jnp.concatenate([b[p] for p in range(3) for b in backs], axis=2)
    joint_back = tick(one, joint_back)
    dprojected = [joint_back[:, : padded[0]], joint_back[:, padded[0] :]]
    inward_terms = [
        product("std,stf->df", act[m], dprojected[m]).astype(bfloat16) for m in both
    ]
    inward_terms = tick(two, inward_terms)
    sums[0].queue(*add_terms(inward_terms[:1], 1)).begin()
    sums[1].queue(*add_terms(inward_terms[1:], -1)).begin()
    dact_flow = Flow(
        col_scatter_rounds(
            [product("stf,df->std", dprojected[m], inward[m])[:, : lengths[m]] for m in both]
        )
    )
    outputs = [
        (middle[m] + component(mods[m], 5) * mlp_out[m]).astype(bfloat16).reshape(-1, local_width)
        for m in both
    ]
    early = [
        [
            jnp.sum(dmiddle[m] * branch[m], axis=1),
            jnp.sum(dmlp_in[m], axis=1),
            jnp.sum(dmlp_in[m] * normed_two[m], axis=1),
            jnp.sum(cotangents[m] * mlp_out[m], axis=1),
        ]
        for m in both
    ]
    tick([dact_flow, sums[1]])
    early, outputs = tick(one, (early, outputs))
    tick([dact_flow, sums[1]])
    dact = finish(dact_flow)
    normed_one = [(inputs[m] - first[m][0]) * first[m][1] for m in both]
    upward = [dact[m] * (1.0 + component(mods[m], 1)) for m in both]
    norm_flow = Flow(
        col_sum_rounds(
            jnp.stack(
                [
                    jnp.concatenate([jnp.sum(upward[m], axis=2) for m in both], axis=1),
                    jnp.concatenate(
                        [jnp.sum(upward[m] * normed_one[m], axis=2) for m in both], axis=1
                    ),
                ]
            )
        )
    )
    dmods = jnp.stack(
        [
            jnp.stack(
                [
                    jnp.sum(dact[m], axis=1),
                    jnp.sum(dact[m] * normed_one[m], axis=1),
                    *early[m],
                ],
                axis=1,
            )
            for m in both
        ],
        axis=1,
    ).astype(bfloat16)
    dmod_flow = Flow(row_gather_rounds(dmods))
    tick([norm_flow, sums[0]])
    tick([norm_flow, dmod_flow, sums[1]])
    totals = finish(norm_flow) / features
    means = [totals[:, :, : lengths[0], None], totals[:, :, lengths[0] :, None]]
    input_grads = [
        (
            dmiddle[m]
            + first[m][1] * (upward[m] - means[m][0] - normed_one[m] * means[m][1])
        ).reshape(-1, local_width)
        for m in both
    ]
    input_grads = tick([sums[0], dmod_flow], input_grads)
    tick([sums[1], dmod_flow])
    dmods_all = finish(dmod_flow)
    mod_grads = [product("rsd,rskf->dkf", cond_mine, dmods_all[:, :, m]) for m in both]
    mod_grads = tick(one, mod_grads)
    for flow in sums:
        finish(flow)
    contract_sums, outward_sums, image_sums = sums[0].results
    expand_sums, text_sums = sums[1].results
    return (
        *outputs,
        *input_grads,
        *mod_grads,
        *[v[0].reshape(-1, 3, local_width) for v in (image_sums, text_sums)],
        *[outward_sums[m].T for m in both],
        *[expand_sums[m] for m in both],
        *[contract_sums[m].T for m in both],
    )


def solution(mesh):
    placed = (
        P("row", "col"),
        P("row", "col"),
        P("row", None),
        P("row", None),
        P("row", None, "col"),
        P("row", None, "col"),
        P("row", None, "col"),
        P("row", None, "col"),
        P("col", "row"),
        P("col", "row"),
        P("row", "col"),
        P("row", "col"),
        P("col", "row"),
        P("col", "row"),
        P("row", "col"),
        P("row", "col"),
    )
    return jax.shard_map(
        local,
        mesh=mesh,
        in_specs=placed,
        out_specs=(
            P("row", "col"),
            P("row", "col"),
            P("row", "col"),
            P("row", "col"),
            P("row", None, "col"),
            P("row", None, "col"),
            P("row", None, "col"),
            P("row", None, "col"),
            P("col", "row"),
            P("col", "row"),
            P("row", "col"),
            P("row", "col"),
            P("col", "row"),
            P("col", "row"),
        ),
        check_vma=False,
    )
```
